256 devices in a mesh: wide: 32 (over x, y, core), narrow: 8 (over z).
Axes of the slice: x: 4, y: 4, z: 8, core: 2. Of those that a mesh axis runs over, the one named last changes fastest.
Arguments:
- decode_hidden_input: bfloat16 [1024, 8192], P('wide'), may hold values from -6 to 6
- queries: bfloat16 [1024, 8192], P('wide', 'narrow'), may hold values from -8 to 8
- cached_key_rows: bfloat16 [1024, 256, 1024], P('wide', None, 'narrow'), may hold values from -4 to 4
- cached_value_rows: bfloat16 [1024, 256, 1024], P('wide', None, 'narrow'), may hold values from -6 to 6
- lengths: int32 [1024], P('wide'), may hold values from 2 to 256, as said below
- decode_adapter_index: int32 [1024], P('wide'), may hold values from 0 to 511, as said below
- key_matrix: bfloat16 [8192, 1024], P(None, 'narrow'), may hold values from -0.0625 to 0.0625
- value_matrix: bfloat16 [8192, 1024], P(None, 'narrow'), may hold values from -0.0625 to 0.0625
- adapter_down_map: bfloat16 [512, 16, 8192], P('wide', None, 'narrow'), may hold values from -0.0625 to 0.0625
- adapter_up_map: bfloat16 [512, 16, 1024], P('wide', None, 'narrow'), may hold values from -0.1875 to 0.1875
- training_hidden_input: bfloat16 [32768, 8192], P('wide', 'narrow'), may hold values from -6 to 6
- cotangent: bfloat16 [32768, 1024], P('wide', 'narrow'), may hold values from -0.3984375 to 0.3984375
- training_adapter_index: int32 [32768], P('wide'), may hold values from 0 to 511, as said below
- rewards: int32 [32768], P('wide'), may hold values from -2 to 2
Outputs:
- attended: bfloat16 [1024, 8192], P('wide', 'narrow')
- fresh_values: bfloat16 [1024, 1024], P('wide', 'narrow')
- grad_down: float32 [512, 16, 8192], P('wide', None, 'narrow')
- grad_up: float32 [512, 16, 1024], P('wide', None, 'narrow')
The draws below stay inside these ranges and needn't reach their ends.
Inputs may be any that keep to these rules, and one draw needn't show every extreme that they name: `decode_adapter_index`: of the 32 rows of one index of wide, at most 2 use adapters of one owner (adapters o * 16 to (o + 1) * 16 - 1); in every draw one owner gets exactly 2 rows from every index of wide. `training_adapter_index`: of the 1024 tokens of one index of wide, at most 64 use adapters of one owner (adapters o * 16 to (o + 1) * 16 - 1); in every draw one owner gets exactly 64 tokens from every index of wide. `lengths`: every block of 32 rows holds a row of length 256.
All inputs are finite; a program needn't handle non-finite values.
Results may differ from the reference program's by a relative error of at most 0.0051.
Values may be sent and summed in bfloat16 or wider, within the bound.
A program may use at most 64 MiB of HBM per device.

```python
import math
import jax
import jax.numpy as jnp
from jax import lax

MODEL_WIDTH = 8192
HEADS = 64
KEY_VALUE_HEADS = 8
HEAD_SIZE = 128
ADAPTER_RANK = 16
ADP_DEV = 16
ROW_DEV = 32
TOK_DEV = 1024
CACHE = 256
ADAPTER_COUNT = 512
ROWS = 1024
TOKENS = 32768


def route_draw(key, blocks, rows, owners, owner_totals, salt):
    capacity = 2 * rows // owners
    slots = owners * capacity
    popular_key, block_key = jax.random.split(jax.random.fold_in(key, salt))
    standing = jax.random.permutation(popular_key, owners).astype(jnp.int32)
    slot_owner = jnp.arange(slots, dtype=jnp.int32) // capacity
    slot_rank = standing[slot_owner]

    def one_block(subkey):
        noise_key, order_key, local_key, mixing_key = jax.random.split(subkey, 4)
        noise_value = jax.random.randint(noise_key, (slots,), 0, 64).astype(jnp.int32)
        tiebreak = jax.random.permutation(order_key, slots).astype(jnp.int32)
        favour = jnp.where(slot_rank == owners - 1, 1024, 0).astype(jnp.int32)
        score = (noise_value + slot_rank * 4 + favour) * slots + tiebreak
        chosen = lax.top_k(score, rows)[1].astype(jnp.int32)
        owner_pick = chosen // capacity
        local_pick = jax.random.randint(local_key, (rows,), 0, owner_totals).astype(jnp.int32)
        picked = owner_pick * owner_totals + local_pick
        return picked[jax.random.permutation(mixing_key, rows)]
    drawn = jax.vmap(one_block)(jax.random.split(block_key, blocks))
    return drawn.reshape(-1).astype(jnp.int32)


def draw_decode_adapter_index(key, part):
    return route_draw(key, ROWS // ROW_DEV, ROW_DEV, ROWS // ROW_DEV, ADP_DEV, 7)


def draw_training_adapter_index(key, part):
    return route_draw(key, TOKENS // TOK_DEV, TOK_DEV, TOKENS // TOK_DEV, ADP_DEV, 11)


def draw_lengths(key, part):
    first_key, second_key = jax.random.split(jax.random.fold_in(key, 13))
    drawn = jax.random.randint(first_key, (ROWS,), 2, CACHE + 1).astype(jnp.int32)
    blocks = ROWS // ROW_DEV
    longest = jax.random.randint(second_key, (blocks,), 0, ROW_DEV).astype(jnp.int32)
    filled = (jnp.arange(ROW_DEV, dtype=jnp.int32)[None, :] == longest[:, None]).reshape(-1)
    return jnp.where(filled, CACHE, drawn).astype(jnp.int32)


def drawn_pair(key):
    key_part, query_part = jax.random.split(jax.random.fold_in(key, 29))
    group = HEADS // KEY_VALUE_HEADS
    key_shape = (ROWS, CACHE, KEY_VALUE_HEADS, HEAD_SIZE)
    query_shape = (ROWS, KEY_VALUE_HEADS, group, HEAD_SIZE)
    key_draw = jnp.clip(jax.random.normal(key_part, key_shape, jnp.float32), -4.0, 4.0)
    query_draw = jnp.clip(jax.random.normal(query_part, query_shape, jnp.float32), -8.0, 8.0)
    return (key_draw.reshape(ROWS, CACHE, KEY_VALUE_HEADS * HEAD_SIZE), query_draw.reshape(ROWS, HEADS * HEAD_SIZE))


def draw_cached_key_rows(key, part):
    return drawn_pair(key)[0].astype(jnp.bfloat16)


def draw_queries(key, part):
    return drawn_pair(key)[1].astype(jnp.bfloat16)


def place_ends(entries, key, smallest, high):
    longest = entries.shape.index(max(entries.shape))
    spots = []
    for shift in (0, 1):
        where = [jax.random.randint(jax.random.fold_in(key, axis), (), 0, length) for axis, length in enumerate(entries.shape)]
        where[longest] = (where[longest] + shift) % entries.shape[longest]
        spots.append(tuple(where))
    return entries.at[spots[0]].set(smallest).at[spots[1]].set(high)


def block_levels(rng, extent, shards, least, top_value):
    def one(position, shards_of):
        steps = jax.random.uniform(jax.random.fold_in(jax.random.fold_in(rng, 6), position), (shards_of,), jnp.float32, least / len(shards), top_value / len(shards))
        return jnp.repeat(jnp.exp(steps), extent[position] // shards_of).reshape((-1,) + (1,) * (len(extent) - position - 1))

    loudness = one(*shards[0])
    for cut in shards[1:]:
        loudness = loudness * one(*cut)
    return loudness


def noise(rng, dims, deviation, bound, cuts=(), kind=jnp.bfloat16):
    values = jax.random.normal(rng, dims, jnp.float32) * deviation
    if len(cuts) > 0:
        values = block_levels(rng, dims, cuts, -0.22, 0.18) * values
    return jnp.clip(values, min=-bound, max=bound).astype(kind)


def setup_inputs(seed: int = 0) -> dict:
    arg_keys = jax.random.split(jax.random.key(seed), 15)
    return {
        "decode_hidden_input": noise(arg_keys[0], (ROWS, MODEL_WIDTH), 1.0, 6.0, ((0, 32),)),
        "queries": draw_queries(jax.random.fold_in(arg_keys[14], 71), 0),
        "cached_key_rows": draw_cached_key_rows(jax.random.fold_in(arg_keys[14], 71), 0),
        "cached_value_rows": noise(arg_keys[3], (ROWS, CACHE, KEY_VALUE_HEADS * HEAD_SIZE), 1.0, 6.0, ((0, 32), (2, 8))),
        "lengths": draw_lengths(jax.random.fold_in(arg_keys[14], 71), 0),
        "decode_adapter_index": draw_decode_adapter_index(jax.random.fold_in(arg_keys[14], 71), 0),
        "key_matrix": noise(arg_keys[6], (MODEL_WIDTH, KEY_VALUE_HEADS * HEAD_SIZE), MODEL_WIDTH ** -0.5, 0.0625, ((1, 8),)),
        "value_matrix": noise(arg_keys[7], (MODEL_WIDTH, KEY_VALUE_HEADS * HEAD_SIZE), MODEL_WIDTH ** -0.5, 0.0625, ((1, 8),)),
        "adapter_down_map": noise(arg_keys[8], (ADAPTER_COUNT, ADAPTER_RANK, MODEL_WIDTH), MODEL_WIDTH ** -0.5, 0.0625, ((0, 32), (2, 8))),
        "adapter_up_map": noise(arg_keys[9], (ADAPTER_COUNT, ADAPTER_RANK, KEY_VALUE_HEADS * HEAD_SIZE), (KEY_VALUE_HEADS * HEAD_SIZE) ** -0.5, 0.1875, ((0, 32), (2, 8))),
        "training_hidden_input": noise(arg_keys[10], (TOKENS, MODEL_WIDTH), 1.0, 6.0, ((0, 32), (1, 8))),
        "cotangent": noise(arg_keys[11], (TOKENS, KEY_VALUE_HEADS * HEAD_SIZE), 0.05, 0.3984375, ((0, 32), (1, 8))),
        "training_adapter_index": draw_training_adapter_index(jax.random.fold_in(arg_keys[14], 71), 0),
        "rewards": place_ends(jax.random.randint(arg_keys[13], (TOKENS,), -2, 3), jax.random.fold_in(arg_keys[13], 1), -2, 2).astype(jnp.int32),
    }


ADAPTER_SCALE = 2.0
NEG_FILL = -1e+30

def attention_block(input_rows, projected_queries, projected_keys, projected_values, row_lengths, adapter_per_row, key_matrix, value_matrix, adapter_down_map, adapter_up_map):
    row_count = input_rows.shape[0]
    group = HEADS // KEY_VALUE_HEADS
    fresh_keys = jnp.dot(input_rows, key_matrix, preferred_element_type=jnp.float32).astype(jnp.bfloat16)
    down_weight_rows = adapter_down_map[adapter_per_row].astype(jnp.float32)
    rank_activations = jnp.einsum('fj,fkj->fk', input_rows.astype(jnp.float32), down_weight_rows).astype(jnp.bfloat16)
    up_weight_rows = adapter_up_map[adapter_per_row].astype(jnp.float32)
    value_delta_rows = (ADAPTER_SCALE * jnp.einsum('xy,xyd->xd', rank_activations.astype(jnp.float32), up_weight_rows)).astype(jnp.bfloat16)
    fresh_values = (jnp.dot(input_rows, value_matrix, preferred_element_type=jnp.float32) + value_delta_rows.astype(jnp.float32)).astype(jnp.bfloat16)
    query_heads = projected_queries.reshape(row_count, KEY_VALUE_HEADS, group, HEAD_SIZE).astype(jnp.float32)
    key_heads = projected_keys.reshape(row_count, CACHE, KEY_VALUE_HEADS, HEAD_SIZE).astype(jnp.float32)
    value_heads = projected_values.reshape(row_count, CACHE, KEY_VALUE_HEADS, HEAD_SIZE).astype(jnp.float32)
    inverse = 1.0 / math.sqrt(HEAD_SIZE)
    scores = jnp.einsum('bhgd,bphd->bhgp', query_heads, key_heads) * inverse
    own_score = jnp.einsum('bhgd,bhd->bhg', query_heads, fresh_keys.reshape(row_count, KEY_VALUE_HEADS, HEAD_SIZE).astype(jnp.float32)) * inverse
    allowed = jnp.arange(CACHE)[None, :] < row_lengths[:, None]
    scores = jnp.where(allowed[:, None, None, :], scores, NEG_FILL)
    highest = jnp.maximum(lax.optimization_barrier(jnp.max(scores, axis=-1)), own_score)
    cache_exp = jnp.exp(scores - highest[..., None])
    own_exp = jnp.exp(own_score - highest)
    denominator = lax.optimization_barrier(jnp.sum(cache_exp, axis=-1)) + own_exp
    cache_weight = (cache_exp / denominator[..., None]).astype(jnp.bfloat16)
    own_weight = (own_exp / denominator).astype(jnp.bfloat16)
    attended = jnp.einsum('bhgp,bphd->bhgd', cache_weight.astype(jnp.float32), value_heads)
    attended = attended + own_weight.astype(jnp.float32)[..., None] * fresh_values.reshape(row_count, KEY_VALUE_HEADS, 1, HEAD_SIZE).astype(jnp.float32)
    return (attended.reshape(row_count, HEADS * HEAD_SIZE).astype(jnp.bfloat16), fresh_values)

def reference(decode_hidden_input, queries, cached_key_rows, cached_value_rows, lengths, decode_adapter_index, key_matrix, value_matrix, adapter_down_map, adapter_up_map, training_hidden_input, cotangent, training_adapter_index, rewards):
    row_block = math.gcd(ROWS, 128)

    def split_rows(array):
        return array.reshape((ROWS // row_block, row_block) + array.shape[1:])

    def decode_piece(split_parts):
        return attention_block(*split_parts, key_matrix, value_matrix, adapter_down_map, adapter_up_map)
    attended, fresh_values = lax.map(decode_piece, (split_rows(decode_hidden_input), split_rows(queries), split_rows(cached_key_rows), split_rows(cached_value_rows), split_rows(lengths), split_rows(decode_adapter_index)))
    attended = attended.reshape(ROWS, HEADS * HEAD_SIZE)
    fresh_values = fresh_values.reshape(ROWS, KEY_VALUE_HEADS * HEAD_SIZE)
    tok_block = math.gcd(TOKENS, 256)

    def split_tokens(array):
        return array.reshape((TOKENS // tok_block, tok_block) + array.shape[1:])

    def train_step(carry, split_parts):
        grad_down, grad_up = carry
        input_rows, incoming_gradient, adapter_per_row, row_rewards = split_parts
        hidden_state = jnp.einsum('fj,fkj->fk', input_rows.astype(jnp.float32), adapter_down_map[adapter_per_row].astype(jnp.float32))
        backward_result = jnp.einsum('ha,hya->hy', incoming_gradient.astype(jnp.float32), adapter_up_map[adapter_per_row].astype(jnp.float32))
        scale_factor = ADAPTER_SCALE * row_rewards.astype(jnp.float32)[:, None]
        scaled_rank = (scale_factor * hidden_state).astype(jnp.bfloat16)
        scaled_back = (scale_factor * backward_result).astype(jnp.bfloat16)
        grad_down = grad_down.at[adapter_per_row].add(jnp.einsum('nr,nd->nrd', scaled_back.astype(jnp.float32), input_rows.astype(jnp.float32)))
        grad_up = grad_up.at[adapter_per_row].add(jnp.einsum('nr,nk->nrk', scaled_rank.astype(jnp.float32), incoming_gradient.astype(jnp.float32)))
        return ((grad_down, grad_up), None)
    start = (jnp.zeros((ADAPTER_COUNT, ADAPTER_RANK, MODEL_WIDTH), jnp.float32), jnp.zeros((ADAPTER_COUNT, ADAPTER_RANK, KEY_VALUE_HEADS * HEAD_SIZE), jnp.float32))
    (grad_down, grad_up), unused = lax.scan(train_step, start, (split_tokens(training_hidden_input), split_tokens(cotangent), split_tokens(training_adapter_index), split_tokens(rewards)))
    return (attended, fresh_values, grad_down, grad_up)
```

```python
import functools
import math

import jax
import jax.numpy as jnp
from jax import lax
from jax.experimental import pallas as pl
from jax.experimental.pallas import tpu as pltpu
from jax.sharding import PartitionSpec as P

MESH = pl.DeviceIdType.MESH
F32 = jnp.float32
BF16 = jnp.bfloat16
I32 = jnp.int32

PAIRS = [
    [(1, 0), (0, 1), (3, 0), (0, 3)],
    [(1, 1), (3, 3), (1, 3), (3, 1)],
    [(2, 1), (1, 2), (2, 3), (3, 2)],
    [(2, 0), (0, 2)],
    [(2, 2)],
]
ORDER = [(0, 0, 0), (0, 0, 1)]
for group in PAIRS:
    for flip in (0, 1):
        ORDER += [(dx, dy, flip) for dx, dy in group]

DEV = 32
ZDEV = 8
ROWS = 32
TOK = 1024
FEAT = 1024
VAL = 128
WIDTH = FEAT + VAL
PIECE = WIDTH + 128
HALF = 32
ADP = 16
RANK = 16
AR = ADP * RANK
CACHE = 256
HEAD = 128
GROUP = 8
MODEL = 8192
UNITS = 8


def dot_nt(a, b):
    return lax.dot_general(a, b, (((1,), (1,)), ((), ())), preferred_element_type=F32)


def dot_nn(a, b):
    return lax.dot_general(a, b, (((1,), (0,)), ((), ())), preferred_element_type=F32)


def dot_tn(a, b):
    return lax.dot_general(a, b, (((0,), (0,)), ((), ())), preferred_element_type=F32)


def iota(shape, dim):
    return lax.broadcasted_iota(I32, shape, dim)


def kernel(
    lens, meta, h_h, q_h, k_h, v_h, wk_h, wv_h, d_h, u_h, x_h, c_h,
    att_o, fv_o, gd_o, gu_o,
    xb, hb, hs, qb, kb, vb, wkb, wvb, db, ub,
    send, recv, onehot, dec_s, zs, zr, cr, zds, zdr, rets, retr,
    q32, att32, ow, fk, bv,
    lsem, ssem, rsem, zssem, zrsem, dssem, drsem, bssem, brsem,
):
    w = lax.axis_index("wide")
    n = lax.axis_index("narrow")
    wx, wy, wc = w // 8, (w // 2) % 4, w % 2

    def pick(k, which):
        if isinstance(k, int):
            return ORDER[k][which]
        total = jnp.int32(0)
        for i, o in enumerate(ORDER):
            if o[which]:
                total = jnp.where(k == i, jnp.int32(o[which]), total)
        return total

    def peer(k, sign=1):
        dx, dy, dc = pick(k, 0), pick(k, 1), pick(k, 2)
        px = (wx + 4 + sign * dx) % 4
        py = (wy + 4 + sign * dy) % 4
        return (px * 4 + py) * 2 + (wc + dc) % 2

    loads = [
        (x_h, xb.at[:, pl.ds(0, FEAT)]),
        (c_h, xb.at[:, pl.ds(FEAT, VAL)]),
        (h_h.at[:, pl.ds(pl.multiple_of(n * FEAT, FEAT), FEAT)], hs.at[pl.ds(0, ROWS)]),
        (h_h, hb),
        (q_h, qb),
        (wk_h, wkb),
        (wv_h, wvb),
        (k_h, kb),
        (v_h, vb),
        (d_h, db),
        (u_h, ub),
    ]
    copies = [pltpu.make_async_copy(s, t, lsem.at[i]) for i, (s, t) in enumerate(loads)]
    for cp in copies:
        cp.start()

    barrier = pltpu.get_barrier_semaphore()

    @pl.loop(1, DEV)
    def _(k):
        pl.semaphore_signal(barrier, inc=1, device_id=(peer(k), n), device_id_type=MESH)

    @pl.loop(1, ZDEV)
    def _(z):
        pl.semaphore_signal(barrier, inc=1, device_id=(w, (n + z) % ZDEV), device_id_type=MESH)

    row = meta[...]
    lower = jnp.where(iota((128, 128), 0) < iota((128, 128), 1), 1.0, 0.0).astype(BF16)
    ones = jnp.ones((128, 128), BF16)
    prefix = jnp.concatenate([lower, ones], axis=1)
    idx, rew = row[0:1], row[1:2]
    owner = lax.shift_right_arithmetic(idx, 4)
    code = (idx & 15) + 1
    ids = iota((DEV, 128), 0)
    blocks = [owner[:, 128 * j : 128 * j + 128] == ids for j in range(TOK // 128)]
    hot = [jnp.where(m, 1.0, 0.0) for m in blocks]
    ranks = dot_nn(jnp.concatenate(hot, axis=0).astype(BF16), prefix)
    base = jnp.zeros((DEV, 128), F32)
    keys = []
    for j in range(TOK // 128):
        part = ranks[DEV * j : DEV * j + DEV]
        before = part[:, :128] + base
        keys.append(jnp.sum(hot[j] * before, axis=0, keepdims=True))
        base = base + part[:, 128:]
    key = owner * 64 + jnp.concatenate(keys, axis=1).astype(I32)
    line = iota((16, TOK), 0)
    codef, rewf = code.astype(F32), rew.astype(F32)
    meta_a = jnp.where(line == 0, codef, jnp.where(line == 1, rewf, 0.0)).astype(BF16)
    meta_b = jnp.where(line == 2, codef, jnp.where(line == 3, rewf, 0.0)).astype(BF16)

    didx = row[2:3, :128]
    downer = lax.shift_right_arithmetic(didx, 4)
    dhot = jnp.where(downer == ids, 1.0, 0.0)
    drank = jnp.sum(dhot * dot_nn(dhot.astype(BF16), lower), axis=0, keepdims=True)
    dkey = downer * 2 + drank.astype(I32)
    order_peer = jnp.zeros((DEV, 128), I32)
    for k in range(DEV):
        order_peer = jnp.where(ids == k, peer(k), order_peer)
    dpack = [jnp.where(dkey == order_peer * 2 + d, 1.0, 0.0) for d in range(2)]
    dpack_f = jnp.concatenate(dpack, axis=0)
    dpack_b = dpack_f.astype(BF16)
    dcode = jnp.where(didx >= 0, (didx & 15) + 1, 0).astype(F32)
    dline = jnp.where(iota((16, 128), 0) == 4, dcode, 0.0).astype(BF16)
    dpad = jnp.concatenate([dpack_f, jnp.zeros((64, 128), F32)], axis=0).astype(BF16)
    dmeta = dot_nt(dline, dpad)

    hs[pl.ds(ROWS, 128 - ROWS)] = jnp.zeros((128 - ROWS, FEAT), BF16)
    copies[2].wait()
    picked = dot_nn(dpack_b, hs[...])
    for j in range(8):
        for d in range(2):
            dec_s[pl.ds(d * 8 + j, DEV, stride=16), :] = picked[
                32 * d : 32 * d + 32, 128 * j : 128 * j + 128
            ]
    copies[0].wait()
    copies[1].wait()
    pl.semaphore_wait(barrier, DEV - 1 + ZDEV - 1)

    def copy_a(k, p):
        return pltpu.make_async_remote_copy(
            src_ref=send.at[0, k],
            dst_ref=recv.at[0, k],
            send_sem=ssem.at[0, k],
            recv_sem=rsem.at[0, k],
            device_id=(p, n),
            device_id_type=MESH,
        )

    def copy_b(k, p):
        return pltpu.make_async_remote_copy(
            src_ref=send.at[1, k, :, pl.ds(0, WIDTH)],
            dst_ref=recv.at[1, k, :, pl.ds(0, WIDTH)],
            send_sem=ssem.at[1, k],
            recv_sem=rsem.at[1, k],
            device_id=(p, n),
            device_id_type=MESH,
        )

    lane = iota((16, 128), 1)
    slot = iota((HALF, TOK), 0)

    @pl.loop(0, DEV // 4)
    def _(q):
        peers = [peer(q * 4 + i) for i in range(4)]
        for half in range(2):
            for i in range(4):
                match = (key - (peers[i] * 64 + half * HALF)) == slot
                onehot[half * 128 + i * HALF : half * 128 + i * HALF + HALF, :] = jnp.where(
                    match, 1.0, 0.0
                ).astype(BF16)
        rows = dot_nn(onehot[...], xb[...]).astype(BF16)
        tile = dot_nt(meta_a, onehot[0:128]) + dot_nt(meta_b, onehot[128:256])
        for i in range(4):
            k = q * 4 + i
            mine = jnp.where((lane >= 32 * i) & (lane < 32 * i + 32), tile, 0.0)
            mine = mine + jnp.where((lane == k) | (lane == k + 32), dmeta, 0.0)
            send[0, k, :, 0:WIDTH] = rows[32 * i : 32 * i + 32]
            send[0, k, 0:16, WIDTH:PIECE] = mine.astype(BF16)
            send[0, k, 16:32, WIDTH:PIECE] = dec_s[
                pl.ds(pl.multiple_of(k * 16, 16), 16), :
            ].astype(BF16)
            send[1, k, :, 0:WIDTH] = rows[128 + 32 * i : 128 + 32 * i + 32]
        for i in range(4):
            k = q * 4 + i

            @pl.when(k > 0)
            def _():
                copy_a(k, peers[i]).start()

    @pl.loop(1, DEV)
    def _(k):
        copy_b(k, peer(k)).start()

    recv[0, 0] = send[0, 0]
    recv[1, 0, :, 0:WIDTH] = send[1, 0, :, 0:WIDTH]

    for i in range(3, 11):
        copies[i].wait()

    def project(j, acc):
        at = pl.ds(pl.multiple_of(j * 1024, 1024), 1024)
        part = hb[:, at]
        return acc[0] + dot_nn(part, wkb[at, :]), acc[1] + dot_nn(part, wvb[at, :])

    zero = jnp.zeros((ROWS, 128), F32)
    keys_new, values_new = lax.fori_loop(0, MODEL // 1024, project, (zero, zero))
    fk[...] = keys_new.astype(BF16).astype(F32)
    bv[...] = values_new
    for g in range(GROUP):
        q32[pl.ds(g, ROWS, stride=GROUP), :] = qb[:, 128 * g : 128 * g + 128].astype(F32)
    inverse = 1.0 / math.sqrt(HEAD)
    many = 4

    @pl.loop(0, ROWS // many)
    def _(t):
        scores, owns = [], []
        for i in range(many):
            b = t * many + i
            query = q32[pl.ds(pl.multiple_of(b * 8, 8), 8), :]
            s = dot_nt(query.astype(BF16), kb[b]) * inverse
            allowed = iota((GROUP, CACHE), 1) < lens[b]
            scores.append(jnp.where(allowed, s, -1e30))
            owns.append(jnp.sum(query * fk[pl.ds(b, 1), :], axis=1, keepdims=True) * inverse)
        s = jnp.concatenate(scores, axis=0)
        own = jnp.concatenate(owns, axis=0)
        highest = jnp.maximum(jnp.max(s, axis=1, keepdims=True), own)
        e = jnp.exp(s - highest)
        eo = jnp.exp(own - highest)
        total = jnp.sum(e, axis=1, keepdims=True) + eo
        weight = (e / total).astype(BF16)
        own_weight = (eo / total).astype(BF16).astype(F32)
        at = pl.ds(pl.multiple_of(t * many * 8, many * 8), many * 8)
        ow[at, :] = jnp.broadcast_to(own_weight, (many * 8, 128))
        for i in range(many):
            b = t * many + i
            att32[pl.ds(pl.multiple_of(b * 8, 8), 8), :] = dot_nn(
                weight[8 * i : 8 * i + 8], vb[b]
            )

    gd_o[...] = jnp.zeros_like(gd_o)
    gu_o[...] = jnp.zeros_like(gu_o)

    def copy_z(u, z):
        return pltpu.make_async_remote_copy(
            src_ref=zs.at[u],
            dst_ref=zr.at[u, z],
            send_sem=zssem.at[u, z],
            recv_sem=zrsem.at[u, z],
            device_id=(w, (n + z) % ZDEV),
            device_id_type=MESH,
        )

    def copy_zd(z):
        return pltpu.make_async_remote_copy(
            src_ref=zds,
            dst_ref=zdr.at[z],
            send_sem=dssem.at[z],
            recv_sem=drsem.at[z],
            device_id=(w, (n + z) % ZDEV),
            device_id_type=MESH,
        )

    def copy_back(k, p):
        return pltpu.make_async_remote_copy(
            src_ref=rets.at[k],
            dst_ref=retr.at[k],
            send_sem=bssem.at[k],
            recv_sem=brsem.at[k],
            device_id=(p, n),
            device_id_type=MESH,
        )

    def arrive(u):
        first = (u % 4) * 8

        @pl.loop(0, 8)
        def _(i):
            k = first + i

            @pl.when(k > 0)
            def _():
                @pl.when(u < 4)
                def _():
                    copy_a(k, peer(k)).wait_recv()

                @pl.when(u >= 4)
                def _():
                    copy_b(k, peer(k)).wait_recv()

    def received(u, lo, hi):
        return recv[u // 4, pl.ds((u % 4) * 8, 8), :, lo:hi].reshape(256, hi - lo)

    def choose(codes, products):
        total = jnp.zeros((RANK, products.shape[1]), F32)
        for a in range(ADP):
            total = total + jnp.where(codes == a + 1.0, products[16 * a : 16 * a + 16], 0.0)
        return total

    def spread(codes, factors):
        return jnp.concatenate(
            [jnp.where(codes == a + 1.0, factors, 0.0) for a in range(ADP)], axis=0
        ).astype(BF16)

    def stage_one(u):
        arrive(u)

        @pl.when(u < 4)
        def _():
            tiles = []
            for quad in range(2):
                total = jnp.zeros((16, 128), F32)
                for i in range(4):
                    total = total + recv[0, u * 8 + quad * 4 + i, 0:16, WIDTH:PIECE].astype(F32)
                tiles.append(total)
            both = jnp.concatenate(tiles, axis=1)
            cr[u, 0:2] = both[0:2]
            cr[u + 4, 0:2] = both[2:4]

        codes = cr[u, 0:1]
        hidden = choose(codes, dot_nt(db[...], received(u, 0, FEAT)))
        back = choose(codes, dot_nt(ub[...], received(u, FEAT, WIDTH)))
        zs[u] = jnp.concatenate([hidden, back], axis=0).astype(BF16)

        @pl.loop(1, ZDEV)
        def _(z):
            copy_z(u, z).start()

    def stage_two(u):
        total = zs[u].astype(F32)
        for z in range(1, ZDEV):
            copy_z(u, z).wait_recv()
            total = total + zr[u, z].astype(F32)
        codes = cr[u, 0:1]
        scaled = (2.0 * cr[u, 1:2]) * total
        scaled = scaled.astype(BF16).astype(F32)
        gd_o[...] += dot_nn(spread(codes, scaled[16:32]), received(u, 0, FEAT))
        gu_o[...] += dot_nn(spread(codes, scaled[0:16]), received(u, FEAT, WIDTH))

    def decode_codes():
        def add(k, acc):
            return acc + recv[0, k, 0:16, WIDTH:PIECE].astype(F32)

        total = lax.fori_loop(0, DEV, add, jnp.zeros((16, 128), F32))
        return jnp.where(iota((1, 128), 1) < 64, total[4:5], 0.0)

    def decode_one():
        @pl.loop(0, DEV)
        def _(k):
            dec_s[pl.ds(pl.multiple_of(k * 16, 16), 16), :] = recv[
                0, k, 16:32, WIDTH:PIECE
            ].astype(F32)

        products = jnp.zeros((AR, 128), F32)
        for j in range(8):
            rows = [dec_s[pl.ds(d * 8 + j, DEV, stride=16), :] for d in range(2)]
            rows = jnp.concatenate(rows + [jnp.zeros((64, 128), F32)], axis=0).astype(BF16)
            products = products + dot_nt(db[:, 128 * j : 128 * j + 128], rows)
        zds[...] = choose(decode_codes(), products)

        @pl.loop(1, ZDEV)
        def _(z):
            copy_zd(z).start()

    def decode_two():
        total = zds[...]
        for z in range(1, ZDEV):
            copy_zd(z).wait_recv()
            total = total + zdr[z]
        total = total.astype(BF16).astype(F32)
        delta = 2.0 * dot_tn(spread(decode_codes(), total), ub[...])
        delta = delta.astype(BF16).astype(F32)
        for d in range(2):
            for k in range(DEV):
                rets[k, d : d + 1, :] = delta[32 * d + k : 32 * d + k + 1]

        @pl.loop(1, DEV)
        def _(k):
            copy_back(k, peer(k, -1)).start()

        retr[0] = rets[0]

    rets[...] = jnp.zeros_like(rets)

    @pl.loop(0, UNITS + 1)
    def _(u):
        @pl.when(u < UNITS)
        def _():
            stage_one(u)

        @pl.when(u > 0)
        def _():
            stage_two(u - 1)

        @pl.when(u == 3)
        def _():
            decode_one()

        @pl.when(u == 4)
        def _():
            decode_two()

    @pl.loop(1, DEV)
    def _(k):
        copy_back(k, peer(k, -1)).wait_recv()

    gathered = jnp.zeros((128, 128), F32)
    for d in range(2):
        mine = jnp.concatenate([retr[k, d : d + 1, :] for k in range(DEV)], axis=0)
        gathered = gathered + dot_tn(dpack[d].astype(BF16), mine.astype(BF16))
    fresh = (bv[...] + gathered[0:ROWS]).astype(BF16)
    fv_o[...] = fresh
    fresh = fresh.astype(F32)
    for g in range(GROUP):
        at = pl.ds(g, ROWS, stride=GROUP)
        att_o[:, 128 * g : 128 * g + 128] = (att32[at, :] + ow[at, :] * fresh).astype(BF16)

    @pl.loop(1, DEV)
    def _(k):
        copy_a(k, peer(k)).wait_send()
        copy_b(k, peer(k)).wait_send()
        copy_back(k, peer(k, -1)).wait_send()

    @pl.loop(1, ZDEV)
    def _(z):
        copy_zd(z).wait_send()

        @pl.loop(0, UNITS)
        def _(u):
            copy_z(u, z).wait_send()


def per_device(
    decode_hidden_input,
    queries,
    cached_key_rows,
    cached_value_rows,
    lengths,
    decode_adapter_index,
    key_matrix,
    value_matrix,
    adapter_down_map,
    adapter_up_map,
    training_hidden_input,
    cotangent,
    training_adapter_index,
    rewards,
):
    decode_row = jnp.pad(decode_adapter_index, (0, TOK - ROWS), constant_values=-1)
    meta = jnp.stack([training_adapter_index, rewards, decode_row] + [rewards] * 5)
    vmem = pl.BlockSpec(memory_space=pltpu.VMEM)
    hbm = pl.BlockSpec(memory_space=pl.ANY)
    dma = pltpu.SemaphoreType.DMA
    attended, fresh, down, up = pl.pallas_call(
        kernel,
        out_shape=(
            jax.ShapeDtypeStruct((ROWS, GROUP * HEAD), BF16),
            jax.ShapeDtypeStruct((ROWS, VAL), BF16),
            jax.ShapeDtypeStruct((AR, FEAT), F32),
            jax.ShapeDtypeStruct((AR, VAL), F32),
        ),
        in_specs=[pl.BlockSpec(memory_space=pltpu.SMEM), vmem] + [hbm] * 10,
        out_specs=(vmem,) * 4,
        scratch_shapes=[
            pltpu.VMEM((TOK, WIDTH), BF16),
            pltpu.VMEM((ROWS, MODEL), BF16),
            pltpu.VMEM((128, FEAT), BF16),
            pltpu.VMEM((ROWS, GROUP * HEAD), BF16),
            pltpu.VMEM((ROWS, CACHE, HEAD), BF16),
            pltpu.VMEM((ROWS, CACHE, HEAD), BF16),
            pltpu.VMEM((MODEL, HEAD), BF16),
            pltpu.VMEM((MODEL, HEAD), BF16),
            pltpu.VMEM((AR, FEAT), BF16),
            pltpu.VMEM((AR, VAL), BF16),
            pltpu.VMEM((2, DEV, HALF, PIECE), BF16),
            pltpu.VMEM((2, DEV, HALF, PIECE), BF16),
            pltpu.VMEM((256, TOK), BF16),
            pltpu.VMEM((512, 128), F32),
            pltpu.VMEM((UNITS, 2 * RANK, 256), BF16),
            pltpu.VMEM((UNITS, ZDEV, 2 * RANK, 256), BF16),
            pltpu.VMEM((UNITS, 8, 256), F32),
            pltpu.VMEM((RANK, 128), F32),
            pltpu.VMEM((ZDEV, RANK, 128), F32),
            pltpu.VMEM((DEV, 8, 128), F32),
            pltpu.VMEM((DEV, 8, 128), F32),
            pltpu.VMEM((ROWS * GROUP, HEAD), F32),
            pltpu.VMEM((ROWS * GROUP, HEAD), F32),
            pltpu.VMEM((ROWS * GROUP, HEAD), F32),
            pltpu.VMEM((ROWS, HEAD), F32),
            pltpu.VMEM((ROWS, HEAD), F32),
            dma((11,)),
            dma((2, DEV)),
            dma((2, DEV)),
            dma((UNITS, ZDEV)),
            dma((UNITS, ZDEV)),
            dma((ZDEV,)),
            dma((ZDEV,)),
            dma((DEV,)),
            dma((DEV,)),
        ],
        compiler_params=pltpu.CompilerParams(
            collective_id=0, has_side_effects=True, vmem_limit_bytes=60 << 20
        ),
    )(
        lengths,
        meta,
        decode_hidden_input,
        queries,
        cached_key_rows,
        cached_value_rows,
        key_matrix,
        value_matrix,
        adapter_down_map.reshape(AR, FEAT),
        adapter_up_map.reshape(AR, VAL),
        training_hidden_input,
        cotangent,
    )
    return attended, fresh, down.reshape(ADP, RANK, FEAT), up.reshape(ADP, RANK, VAL)


def solution(mesh):
    return jax.shard_map(
        per_device,
        mesh=mesh,
        in_specs=(
            P("wide", None),
            P("wide", "narrow"),
            P("wide", None, "narrow"),
            P("wide", None, "narrow"),
            P("wide"),
            P("wide"),
            P(None, "narrow"),
            P(None, "narrow"),
            P("wide", None, "narrow"),
            P("wide", None, "narrow"),
            P("wide", "narrow"),
            P("wide", "narrow"),
            P("wide"),
            P("wide"),
        ),
        out_specs=(
            P("wide", "narrow"),
            P("wide", "narrow"),
            P("wide", None, "narrow"),
            P("wide", None, "narrow"),
        ),
        check_vma=False,
    )
```

```python
import functools
import math

import jax
import jax.numpy as jnp
from jax import lax
from jax.experimental import pallas as pl
from jax.experimental.pallas import tpu as pltpu
from jax.sharding import PartitionSpec as P

MESH = pl.DeviceIdType.MESH
F32 = jnp.float32
BF16 = jnp.bfloat16
I32 = jnp.int32

PAIRS = [
    [(1, 0), (0, 1), (3, 0), (0, 3)],
    [(1, 1), (3, 3), (1, 3), (3, 1)],
    [(2, 1), (1, 2), (2, 3), (3, 2)],
    [(2, 0), (0, 2)],
    [(2, 2)],
]
ORDER = [(0, 0, 0), (0, 0, 1)]
for group in PAIRS:
    for flip in (0, 1):
        ORDER += [(dx, dy, flip) for dx, dy in group]

DEV = 32
ZDEV = 8
ROWS = 32
TOK = 1024
FEAT = 1024
VAL = 128
WIDTH = FEAT + VAL
EXTRA = WIDTH + VAL
PIECE = EXTRA + 128
HALF = 32
ADP = 16
RANK = 16
AR = ADP * RANK
CACHE = 256
HEAD = 128
GROUP = 8
MODEL = 8192
UNITS = 4


def dot_nt(a, b):
    return lax.dot_general(a, b, (((1,), (1,)), ((), ())), preferred_element_type=F32)


def dot_nn(a, b):
    return lax.dot_general(a, b, (((1,), (0,)), ((), ())), preferred_element_type=F32)


def dot_tn(a, b):
    return lax.dot_general(a, b, (((0,), (0,)), ((), ())), preferred_element_type=F32)


def iota(shape, dim):
    return lax.broadcasted_iota(I32, shape, dim)


def kernel(
    lens_h, idx_h, rew_h, didx_h, h_h, q_h, k_h, v_h, wk_h, wv_h, d_h, u_h, x_h, c_h,
    att_o, fv_o, gd_o, gu_o,
    lens, idxb, rewb, didxb, xb, hb, hs, qb, kb, vb, wkb, wvb, db, ub,
    send, recv, onehot, dec_s, zsa, zsb, zra, zrb, cr, later, zds, zdr, rets, retr,
    q32, att32, ow, fk, bv,
    lsem, ssem, rsem, zssem, zrsem, dssem, drsem, bssem, brsem,
):
    w = lax.axis_index("wide")
    n = lax.axis_index("narrow")
    wx, wy, wc = w // 8, (w // 2) % 4, w % 2

    def pick(k, which):
        if isinstance(k, int):
            return ORDER[k][which]
        total = jnp.int32(0)
        for i, o in enumerate(ORDER):
            if o[which]:
                total = jnp.where(k == i, jnp.int32(o[which]), total)
        return total

    def peer(k, sign=1):
        dx, dy, dc = pick(k, 0), pick(k, 1), pick(k, 2)
        px = (wx + 4 + sign * dx) % 4
        py = (wy + 4 + sign * dy) % 4
        return (px * 4 + py) * 2 + (wc + dc) % 2

    loads = [
        (idx_h, idxb),
        (rew_h, rewb),
        (didx_h, didxb),
        (lens_h, lens),
        (x_h, xb.at[:, pl.ds(0, FEAT)]),
        (c_h, xb.at[:, pl.ds(FEAT, VAL)]),
        (h_h.at[:, pl.ds(pl.multiple_of(n * FEAT, FEAT), FEAT)], hs.at[pl.ds(0, ROWS)]),
        (h_h, hb),
        (q_h, qb),
        (wk_h, wkb),
        (wv_h, wvb),
        (k_h, kb),
        (v_h, vb),
        (d_h, db),
        (u_h, ub),
    ]
    copies = [pltpu.make_async_copy(s, t, lsem.at[i]) for i, (s, t) in enumerate(loads)]
    for cp in copies[:7]:
        cp.start()

    barrier = pltpu.get_barrier_semaphore()

    for k in range(1, DEV):
        pl.semaphore_signal(barrier, inc=1, device_id=(peer(k), n), device_id_type=MESH)
    for z in range(1, ZDEV):
        pl.semaphore_signal(barrier, inc=1, device_id=(w, (n + z) % ZDEV), device_id_type=MESH)

    hs[pl.ds(ROWS, 128 - ROWS)] = jnp.zeros((128 - ROWS, FEAT), BF16)
    lower = jnp.where(iota((128, 128), 0) < iota((128, 128), 1), 1.0, 0.0).astype(BF16)
    ones = jnp.ones((128, 128), BF16)
    prefix = jnp.concatenate([lower, ones], axis=1)
    for cp in copies[:4]:
        cp.wait()
    idx = jnp.concatenate([idxb[j : j + 1, :] for j in range(8)], axis=1)
    rew = jnp.concatenate([rewb[j : j + 1, :] for j in range(8)], axis=1)
    owner = lax.shift_right_arithmetic(idx, 4)
    code = (idx & 15) + 1
    ids = iota((DEV, 128), 0)
    blocks = [owner[:, 128 * j : 128 * j + 128] == ids for j in range(TOK // 128)]
    hot = [jnp.where(m, 1.0, 0.0) for m in blocks]
    ranks = dot_nn(jnp.concatenate(hot, axis=0).astype(BF16), prefix)
    base = jnp.zeros((DEV, 128), F32)
    keys = []
    for j in range(TOK // 128):
        part = ranks[DEV * j : DEV * j + DEV]
        before = part[:, :128] + base
        keys.append(jnp.sum(hot[j] * before, axis=0, keepdims=True))
        base = base + part[:, 128:]
    key = owner * 64 + jnp.concatenate(keys, axis=1).astype(I32)
    line = iota((16, TOK), 0)
    codef, rewf = code.astype(F32), rew.astype(F32)
    meta_a = jnp.where(line == 0, codef, jnp.where(line == 1, rewf, 0.0)).astype(BF16)
    meta_b = jnp.where(line == 2, codef, jnp.where(line == 3, rewf, 0.0)).astype(BF16)

    didx = jnp.concatenate([didxb[...], jnp.full((1, 96), -1, I32)], axis=1)
    downer = lax.shift_right_arithmetic(didx, 4)
    dhot = jnp.where(downer == ids, 1.0, 0.0)
    drank = jnp.sum(dhot * dot_nn(dhot.astype(BF16), lower), axis=0, keepdims=True)
    dkey = downer * 2 + drank.astype(I32)
    order_peer = jnp.zeros((DEV, 128), I32)
    for k in range(DEV):
        order_peer = jnp.where(ids == k, peer(k), order_peer)
    dpack = [jnp.where(dkey == order_peer * 2 + d, 1.0, 0.0) for d in range(2)]
    dpack_f = jnp.concatenate(dpack, axis=0)
    dpack_b = dpack_f.astype(BF16)
    dcode = jnp.where(didx >= 0, (didx & 15) + 1, 0).astype(F32)
    dline = jnp.where(iota((16, 128), 0) == 4, dcode, 0.0).astype(BF16)
    dpad = jnp.concatenate([dpack_f, jnp.zeros((64, 128), F32)], axis=0).astype(BF16)
    dmeta = dot_nt(dline, dpad)

    copies[6].wait()
    picked = dot_nn(dpack_b, hs[...])
    for j in range(8):
        for d in range(2):
            dec_s[pl.ds(d * 8 + j, DEV, stride=16), :] = picked[
                32 * d : 32 * d + 32, 128 * j : 128 * j + 128
            ]
    copies[4].wait()
    copies[5].wait()
    for cp in copies[7:]:
        cp.start()
    pl.semaphore_wait(barrier, DEV - 1 + ZDEV - 1)

    def copy_a(k, p):
        return pltpu.make_async_remote_copy(
            src_ref=send.at[0, k],
            dst_ref=recv.at[0, k],
            send_sem=ssem.at[0, k],
            recv_sem=rsem.at[0, k],
            device_id=(p, n),
            device_id_type=MESH,
        )

    def copy_b(k, p):
        return pltpu.make_async_remote_copy(
            src_ref=send.at[1, k, :, pl.ds(0, FEAT)],
            dst_ref=recv.at[1, k, :, pl.ds(0, FEAT)],
            send_sem=ssem.at[1, k],
            recv_sem=rsem.at[1, k],
            device_id=(p, n),
            device_id_type=MESH,
        )

    lane = iota((16, 128), 1)
    slot = iota((HALF, TOK), 0)

    @pl.loop(0, DEV // 4)
    def _(q):
        peers = [peer(q * 4 + i) for i in range(4)]
        for half in range(2):
            for i in range(4):
                match = (key - (peers[i] * 64 + half * HALF)) == slot
                onehot[half * 128 + i * HALF : half * 128 + i * HALF + HALF, :] = jnp.where(
                    match, 1.0, 0.0
                ).astype(BF16)
        rows = dot_nn(onehot[...], xb[...]).astype(BF16)
        tile = dot_nt(meta_a, onehot[0:128]) + dot_nt(meta_b, onehot[128:256])
        for i in range(4):
            k = q * 4 + i
            mine = jnp.where((lane >= 32 * i) & (lane < 32 * i + 32), tile, 0.0)
            mine = mine + jnp.where((lane == k) | (lane == k + 32), dmeta, 0.0)
            send[0, k, :, 0:WIDTH] = rows[32 * i : 32 * i + 32]
            send[0, k, 0:16, EXTRA:PIECE] = mine.astype(BF16)
            send[0, k, 16:32, EXTRA:PIECE] = dec_s[
                pl.ds(pl.multiple_of(k * 16, 16), 16), :
            ].astype(BF16)
            send[0, k, :, WIDTH:EXTRA] = rows[128 + 32 * i : 128 + 32 * i + 32, FEAT:]
            send[1, k, :, 0:FEAT] = rows[128 + 32 * i : 128 + 32 * i + 32, :FEAT]
        for i in range(4):
            k = q * 4 + i

            @pl.when(k > 0)
            def _():
                copy_a(k, peers[i]).start()

    @pl.loop(1, DEV)
    def _(k):
        copy_b(k, peer(k)).start()

    recv[0, 0] = send[0, 0]
    recv[1, 0, :, 0:FEAT] = send[1, 0, :, 0:FEAT]

    for i in range(7, 15):
        copies[i].wait()

    def project(j, acc):
        at = pl.ds(pl.multiple_of(j * 1024, 1024), 1024)
        part = hb[:, at]
        return acc[0] + dot_nn(part, wkb[at, :]), acc[1] + dot_nn(part, wvb[at, :])

    zero = jnp.zeros((ROWS, 128), F32)
    keys_new, values_new = lax.fori_loop(0, MODEL // 1024, project, (zero, zero))
    fk[...] = keys_new.astype(BF16).astype(F32)
    bv[...] = values_new
    for g in range(GROUP):
        q32[pl.ds(g, ROWS, stride=GROUP), :] = qb[:, 128 * g : 128 * g + 128].astype(F32)
    inverse = 1.0 / math.sqrt(HEAD)
    many = 4

    @pl.loop(0, ROWS // many)
    def _(t):
        scores, owns = [], []
        for i in range(many):
            b = t * many + i
            query = q32[pl.ds(pl.multiple_of(b * 8, 8), 8), :]
            s = dot_nt(query.astype(BF16), kb[b]) * inverse
            allowed = iota((GROUP, CACHE), 1) < lens[b]
            scores.append(jnp.where(allowed, s, -1e30))
            owns.append(jnp.sum(query * fk[pl.ds(b, 1), :], axis=1, keepdims=True) * inverse)
        s = jnp.concatenate(scores, axis=0)
        own = jnp.concatenate(owns, axis=0)
        highest = jnp.maximum(jnp.max(s, axis=1, keepdims=True), own)
        e = jnp.exp(s - highest)
        eo = jnp.exp(own - highest)
        total = jnp.sum(e, axis=1, keepdims=True) + eo
        weight = (e / total).astype(BF16)
        own_weight = (eo / total).astype(BF16).astype(F32)
        at = pl.ds(pl.multiple_of(t * many * 8, many * 8), many * 8)
        ow[at, :] = jnp.broadcast_to(own_weight, (many * 8, 128))
        for i in range(many):
            b = t * many + i
            att32[pl.ds(pl.multiple_of(b * 8, 8), 8), :] = dot_nn(
                weight[8 * i : 8 * i + 8], vb[b]
            )

    gd_o[...] = jnp.zeros_like(gd_o)
    gu_o[...] = jnp.zeros_like(gu_o)

    def copy_z(u, z, half):
        src, dst = ((zsa, zra), (zsb, zrb))[half]
        return pltpu.make_async_remote_copy(
            src_ref=src.at[u],
            dst_ref=dst.at[u, z],
            send_sem=zssem.at[half, u, z],
            recv_sem=zrsem.at[half, u, z],
            device_id=(w, (n + z) % ZDEV),
            device_id_type=MESH,
        )

    def copy_zd(z):
        return pltpu.make_async_remote_copy(
            src_ref=zds,
            dst_ref=zdr.at[z],
            send_sem=dssem.at[z],
            recv_sem=drsem.at[z],
            device_id=(w, (n + z) % ZDEV),
            device_id_type=MESH,
        )

    def copy_back(k, p):
        return pltpu.make_async_remote_copy(
            src_ref=rets.at[pl.ds(pl.multiple_of(k * 8, 8), 8)],
            dst_ref=retr.at[pl.ds(pl.multiple_of(k * 8, 8), 8)],
            send_sem=bssem.at[k],
            recv_sem=brsem.at[k],
            device_id=(p, n),
            device_id_type=MESH,
        )

    def received(half, u, lo, hi):
        return recv[half, pl.ds(u * 8, 8), :, lo:hi].reshape(256, hi - lo)

    def choose(codes, products):
        total = jnp.zeros((RANK, products.shape[1]), F32)
        for a in range(ADP):
            total = total + jnp.where(codes == a + 1.0, products[16 * a : 16 * a + 16], 0.0)
        return total

    def spread(codes, factors):
        return jnp.concatenate(
            [jnp.where(codes == a + 1.0, factors, 0.0) for a in range(ADP)], axis=0
        ).astype(BF16)

    def early_one(u):
        @pl.loop(0, 8)
        def _(i):
            k = u * 8 + i

            @pl.when(k > 0)
            def _():
                copy_a(k, 0).wait_recv()

        tiles = []
        for quad in range(2):
            part = recv[0, pl.ds(u * 8 + quad * 4, 4), 0:16, EXTRA:PIECE].astype(F32)
            tiles.append(jnp.sum(part, axis=0))
        cr[u, 0:4] = jnp.concatenate(tiles, axis=1)[0:4]
        hidden = choose(cr[u, 0:1], dot_nt(db[...], received(0, u, 0, FEAT)))
        back = choose(cr[u, 0:1], dot_nt(ub[...], received(0, u, FEAT, WIDTH)))
        back_late = choose(cr[u, 2:3], dot_nt(ub[...], received(0, u, WIDTH, EXTRA)))
        zsa[u] = jnp.concatenate([hidden, back, back_late], axis=0).astype(BF16)
        for z in range(1, ZDEV):
            copy_z(u, z, 0).start()

    def early_two(u):
        total = zsa[u].astype(F32)
        for z in range(1, ZDEV):
            copy_z(u, z, 0).wait_recv()
            total = total + zra[u, z].astype(F32)
        codes = cr[u, 0:1]
        scaled = ((2.0 * cr[u, 1:2]) * total[0:32]).astype(BF16).astype(F32)
        later[u] = ((2.0 * cr[u, 3:4]) * total[32:48]).astype(BF16).astype(F32)
        gd_o[...] += dot_nn(spread(codes, scaled[16:32]), received(0, u, 0, FEAT))
        gu_o[...] += dot_nn(spread(codes, scaled[0:16]), received(0, u, FEAT, WIDTH))

    def late_one(u):
        @pl.loop(0, 8)
        def _(i):
            k = u * 8 + i

            @pl.when(k > 0)
            def _():
                copy_b(k, 0).wait_recv()

        codes = cr[u, 2:3]
        rows = received(1, u, 0, FEAT)
        zsb[u] = choose(codes, dot_nt(db[...], rows)).astype(BF16)
        for z in range(1, ZDEV):
            copy_z(u, z, 1).start()
        gd_o[...] += dot_nn(spread(codes, later[u]), rows)

    def late_two(u):
        total = zsb[u].astype(F32)
        for z in range(1, ZDEV):
            copy_z(u, z, 1).wait_recv()
            total = total + zrb[u, z].astype(F32)
        scaled = ((2.0 * cr[u, 3:4]) * total).astype(BF16).astype(F32)
        gu_o[...] += dot_nn(spread(cr[u, 2:3], scaled), received(0, u, WIDTH, EXTRA))

    def decode_codes():
        total = jnp.sum(recv[0, :, 0:16, EXTRA:PIECE].astype(F32), axis=0)
        return jnp.where(iota((1, 128), 1) < 64, total[4:5], 0.0)

    def decode_one():
        dec_s[...] = recv[0, :, 16:32, EXTRA:PIECE].astype(F32).reshape(512, 128)
        products = jnp.zeros((AR, 128), F32)
        for j in range(8):
            rows = [dec_s[pl.ds(d * 8 + j, DEV, stride=16), :] for d in range(2)]
            rows = jnp.concatenate(rows + [jnp.zeros((64, 128), F32)], axis=0).astype(BF16)
            products = products + dot_nt(db[:, 128 * j : 128 * j + 128], rows)
        zds[...] = choose(decode_codes(), products)
        for z in range(1, ZDEV):
            copy_zd(z).start()

    def decode_two():
        total = zds[...]
        for z in range(1, ZDEV):
            copy_zd(z).wait_recv()
            total = total + zdr[z]
        total = total.astype(BF16).astype(F32)
        delta = 2.0 * dot_tn(spread(decode_codes(), total), ub[...])
        delta = delta.astype(BF16).astype(F32)
        for d in range(2):
            rets[pl.ds(d, DEV, stride=8), :] = delta[32 * d : 32 * d + 32]
        for k in range(1, DEV):
            copy_back(k, peer(k, -1)).start()
        retr[0:8] = rets[0:8]

    def decode_three():
        @pl.loop(1, DEV)
        def _(k):
            copy_back(k, 0).wait_recv()

        gathered = jnp.zeros((128, 128), F32)
        for d in range(2):
            mine = retr[pl.ds(d, DEV, stride=8), :].astype(BF16)
            gathered = gathered + dot_tn(dpack[d].astype(BF16), mine)
        fresh = (bv[...] + gathered[0:ROWS]).astype(BF16)
        fv_o[...] = fresh
        fresh = fresh.astype(F32)
        for g in range(GROUP):
            at = pl.ds(g, ROWS, stride=GROUP)
            att_o[:, 128 * g : 128 * g + 128] = (att32[at, :] + ow[at, :] * fresh).astype(BF16)

    rets[...] = jnp.zeros_like(rets)

    @pl.loop(0, UNITS)
    def _(u):
        early_one(u)

        @pl.when(u > 0)
        def _():
            early_two(u - 1)

    decode_one()
    early_two(UNITS - 1)
    decode_two()

    @pl.loop(0, UNITS)
    def _(u):
        late_one(u)

        @pl.when(u > 0)
        def _():
            late_two(u - 1)

    decode_three()
    late_two(UNITS - 1)

    @pl.loop(1, DEV)
    def _(k):
        copy_a(k, 0).wait_send()
        copy_b(k, 0).wait_send()
        copy_back(k, 0).wait_send()

    @pl.loop(1, ZDEV)
    def _(z):
        copy_zd(z).wait_send()

        @pl.loop(0, UNITS)
        def _(u):
            copy_z(u, z, 0).wait_send()
            copy_z(u, z, 1).wait_send()


def hand_over(a, b, c, d, ao, bo, co, do, sem):
    pairs = [(c, co), (a, ao), (d, do), (b, bo)]
    copies = [pltpu.make_async_copy(s, t, sem.at[i]) for i, (s, t) in enumerate(pairs)]
    for cp in copies:
        cp.start()
    for cp in copies:
        cp.wait()


def per_device(
    decode_hidden_input,
    queries,
    cached_key_rows,
    cached_value_rows,
    lengths,
    decode_adapter_index,
    key_matrix,
    value_matrix,
    adapter_down_map,
    adapter_up_map,
    training_hidden_input,
    cotangent,
    training_adapter_index,
    rewards,
):
    vmem = pl.BlockSpec(memory_space=pltpu.VMEM)
    hbm = pl.BlockSpec(memory_space=pltpu.HBM)
    dma = pltpu.SemaphoreType.DMA
    results = pl.pallas_call(
        kernel,
        out_shape=(
            jax.ShapeDtypeStruct((ROWS, GROUP * HEAD), BF16),
            jax.ShapeDtypeStruct((ROWS, VAL), BF16),
            jax.ShapeDtypeStruct((AR, FEAT), F32),
            jax.ShapeDtypeStruct((AR, VAL), F32),
        ),
        in_specs=[hbm] * 14,
        out_specs=(vmem,) * 4,
        scratch_shapes=[
            pltpu.SMEM((ROWS,), I32),
            pltpu.VMEM((8, 128), I32),
            pltpu.VMEM((8, 128), I32),
            pltpu.VMEM((1, ROWS), I32),
            pltpu.VMEM((TOK, WIDTH), BF16),
            pltpu.VMEM((ROWS, MODEL), BF16),
            pltpu.VMEM((128, FEAT), BF16),
            pltpu.VMEM((ROWS, GROUP * HEAD), BF16),
            pltpu.VMEM((ROWS, CACHE, HEAD), BF16),
            pltpu.VMEM((ROWS, CACHE, HEAD), BF16),
            pltpu.VMEM((MODEL, HEAD), BF16),
            pltpu.VMEM((MODEL, HEAD), BF16),
            pltpu.VMEM((AR, FEAT), BF16),
            pltpu.VMEM((AR, VAL), BF16),
            pltpu.VMEM((2, DEV, HALF, PIECE), BF16),
            pltpu.VMEM((2, DEV, HALF, PIECE), BF16),
            pltpu.VMEM((256, TOK), BF16),
            pltpu.VMEM((512, 128), F32),
            pltpu.VMEM((UNITS, 3 * RANK, 256), BF16),
            pltpu.VMEM((UNITS, RANK, 256), BF16),
            pltpu.VMEM((UNITS, ZDEV, 3 * RANK, 256), BF16),
            pltpu.VMEM((UNITS, ZDEV, RANK, 256), BF16),
            pltpu.VMEM((UNITS, 8, 256), F32),
            pltpu.VMEM((UNITS, RANK, 256), F32),
            pltpu.VMEM((RANK, 128), F32),
            pltpu.VMEM((ZDEV, RANK, 128), F32),
            pltpu.VMEM((DEV * 8, 128), F32),
            pltpu.VMEM((DEV * 8, 128), F32),
            pltpu.VMEM((ROWS * GROUP, HEAD), F32),
            pltpu.VMEM((ROWS * GROUP, HEAD), F32),
            pltpu.VMEM((ROWS * GROUP, HEAD), F32),
            pltpu.VMEM((ROWS, HEAD), F32),
            pltpu.VMEM((ROWS, HEAD), F32),
            dma((15,)),
            dma((2, DEV)),
            dma((2, DEV)),
            dma((2, UNITS, ZDEV)),
            dma((2, UNITS, ZDEV)),
            dma((ZDEV,)),
            dma((ZDEV,)),
            dma((DEV,)),
            dma((DEV,)),
        ],
        compiler_params=pltpu.CompilerParams(
            collective_id=0, has_side_effects=True, vmem_limit_bytes=34 << 20
        ),
    )(*[pltpu.with_memory_space_constraint(a, pltpu.HBM) for a in (
        lengths,
        training_adapter_index.reshape(8, 128),
        rewards.reshape(8, 128),
        decode_adapter_index.reshape(1, ROWS),
        decode_hidden_input,
        queries,
        cached_key_rows,
        cached_value_rows,
        key_matrix,
        value_matrix,
        adapter_down_map.reshape(AR, FEAT),
        adapter_up_map.reshape(AR, VAL),
        training_hidden_input,
        cotangent,
    )])
    attended, fresh, down, up = pl.pallas_call(
        hand_over,
        out_shape=[jax.ShapeDtypeStruct(r.shape, r.dtype) for r in results],
        in_specs=[vmem] * 4,
        out_specs=[hbm] * 4,
        scratch_shapes=[dma((4,))],
        compiler_params=pltpu.CompilerParams(vmem_limit_bytes=4 << 20),
    )(*results)
    return attended, fresh, down.reshape(ADP, RANK, FEAT), up.reshape(ADP, RANK, VAL)


def solution(mesh):
    return jax.shard_map(
        per_device,
        mesh=mesh,
        in_specs=(
            P("wide", None),
            P("wide", "narrow"),
            P("wide", None, "narrow"),
            P("wide", None, "narrow"),
            P("wide"),
            P("wide"),
            P(None, "narrow"),
            P(None, "narrow"),
            P("wide", None, "narrow"),
            P("wide", None, "narrow"),
            P("wide", "narrow"),
            P("wide", "narrow"),
            P("wide"),
            P("wide"),
        ),
        out_specs=(
            P("wide", "narrow"),
            P("wide", "narrow"),
            P("wide", None, "narrow"),
            P("wide", None, "narrow"),
        ),
        check_vma=False,
    )
```
